256 devices in a mesh: gx: 4 (over x), gy: 8 (over z_lo, core), gz: 8 (over z_hi, y).
Axes of the slice: x: 4, y: 4, z: 8 (z_hi: 2, z_lo: 4; z = z_hi * 4 + z_lo), core: 2. Of those that a mesh axis runs over, the one named last changes fastest.
Arguments:
- activations: bfloat16 [64, 32, 64, 1024], P(None, 'gx', 'gy', 'gz'), may hold values from -6 to 6
- preact: bfloat16 [64, 32, 64, 1024], P(None, 'gx', 'gy', 'gz'), may hold values from -6 to 6
- upstream: bfloat16 [64, 32, 64, 1024], P(None, 'gx', 'gy', 'gz'), may hold values from -6 to 6
- master: float32 [110592], P(('gx', 'gy', 'gz')), may hold values from -0.15625 to 0.15625
- first_moment: float32 [110592], P(('gx', 'gy', 'gz')), may hold values from -4 to 4
- second_moment: float32 [110592], P(('gx', 'gy', 'gz')), may hold values from 0.05 to 2
Outputs:
- grad_input: bfloat16 [64, 32, 64, 1024], P(None, 'gx', 'gy', 'gz')
- weight_grad: float32 [110592], P(('gx', 'gy', 'gz'))
- new_master: float32 [110592], P(('gx', 'gy', 'gz'))
- new_first: float32 [110592], P(('gx', 'gy', 'gz'))
- new_second: float32 [110592], P(('gx', 'gy', 'gz'))
The draws below stay inside these ranges and needn't reach their ends.
All inputs are finite; a program needn't handle non-finite values.
Results may differ from the reference program's by a relative error of at most 0.0049.
Values may be sent and summed in bfloat16 or wider, within the bound.
A program may use at most 64 MiB of HBM per device.

```python
import math
import jax
import jax.numpy as jnp
from jax import lax

C = 64
NX = 32
NY = 64
NZ = 1024
PARAMS = 110592


def level_of(key, shape, cuts, low, high):
    def one(position, parts):
        draws = jax.random.uniform(jax.random.fold_in(jax.random.fold_in(key, 6), position), (parts,), jnp.float32, low / len(cuts), high / len(cuts))
        return jnp.repeat(jnp.exp(draws), shape[position] // parts).reshape((-1,) + (1,) * (len(shape) - position - 1))

    gain = one(*cuts[0])
    for cut in cuts[1:]:
        gain = gain * one(*cut)
    return gain


def noise(rng, shape, spread, most, pieces=(), held_as=jnp.bfloat16):
    result = spread * jax.random.normal(rng, shape, jnp.float32)
    if pieces:
        result = result * level_of(rng, shape, pieces, -0.22, 0.18)
    return jnp.clip(result, -most, most).astype(held_as)


def setup_inputs(seed: int = 0) -> dict:
    splits = jax.random.split(jax.random.key(seed), 7)
    activations = noise(splits[0], (C, NX, NY, NZ), 1.0, 6.0, ((1, 4), (2, 8), (3, 8)))
    preact = noise(splits[1], (C, NX, NY, NZ), 1.0, 6.0, ((1, 4), (2, 8), (3, 8)))
    upstream = noise(splits[2], (C, NX, NY, NZ), 1.0, 6.0, ((1, 4), (2, 8), (3, 8)))
    master = noise(splits[3], (PARAMS,), (C * 27) ** -0.5, 0.15625, ((0, 256),), jnp.float32)
    first_moment = noise(splits[4], (PARAMS,), 0.5, 4.0, ((0, 256),), jnp.float32)
    second_moment = jnp.clip(jnp.exp(math.log(2.0) - 3.6888794 * jax.random.uniform(splits[5], (PARAMS,), jnp.float32) ** level_of(splits[5], (PARAMS,), ((0, 256),), -0.2, 0.2)), 0.05, 2.0)
    return dict(activations=activations, preact=preact, upstream=upstream, master=master, first_moment=first_moment, second_moment=second_moment)


def reference(activations, preact, upstream, master, first_moment, second_moment):
    pre_grad = jnp.where(preact > 0, upstream, jnp.zeros_like(upstream))
    kernel = master.astype(jnp.bfloat16).reshape(C, C, 27).astype(jnp.float32)
    widths = ((0, 0), (1, 1), (1, 1), (1, 1))
    padded_grad = jnp.pad(pre_grad, widths)
    padded_input = jnp.pad(activations, widths)

    def plane_step(carry, index):
        grad_slab = lax.dynamic_slice_in_dim(padded_grad, index, 3, 1).astype(jnp.float32)
        input_slab = lax.dynamic_slice_in_dim(padded_input, index, 3, 1).astype(jnp.float32)
        center = lax.dynamic_slice_in_dim(pre_grad, index, 1, 1)[:, 0].astype(jnp.float32)
        plane = jnp.zeros((C, NY, NZ), jnp.float32)
        taps = []
        for shift_x in range(3):
            for shift_y in range(3):
                for shift_z in range(3):
                    tap = shift_x * 9 + shift_y * 3 + shift_z
                    source = grad_slab[:, 2 - shift_x, 2 - shift_y:2 - shift_y + NY, 2 - shift_z:2 - shift_z + NZ]
                    plane = plane + jnp.einsum('oi,oyz->iyz', kernel[:, :, tap], source)
                    window = input_slab[:, shift_x, shift_y:shift_y + NY, shift_z:shift_z + NZ]
                    taps.append(jnp.einsum('oyz,iyz->oi', center, window))
        return (carry + jnp.stack(taps, axis=-1), plane)
    start = jnp.zeros((C, C, 27), jnp.float32)
    total, planes = lax.scan(plane_step, start, jnp.arange(NX, dtype=jnp.int32))
    grad_input = jnp.transpose(planes, (1, 0, 2, 3)).astype(jnp.bfloat16)
    weight_grad = total.reshape(-1) / jnp.sqrt(jnp.float32(NX * NY * NZ))
    new_first = 0.9 * first_moment + 0.1 * weight_grad
    new_second = 0.999 * second_moment + 0.001 * weight_grad * weight_grad
    corr_first = 1.0 - (0.9 ** 10) ** 10
    corr_second = 1.0 - (0.999 ** 10) ** 10
    update = new_first / corr_first / (jnp.sqrt(new_second / corr_second) + 1e-08) + 0.01 * master
    new_master = master - 0.05 * update
    return (grad_input, weight_grad, new_master, new_first, new_second)
```

```python
import functools
import math

import jax
import jax.numpy as jnp
from jax import lax
from jax.experimental import pallas as pl
from jax.experimental.pallas import tpu as pltpu
from jax.sharding import PartitionSpec as P

MESH = pl.DeviceIdType.MESH
BF, F32 = jnp.bfloat16, jnp.float32
GX, GY, GZ = 4, 8, 8
C = 64
SX, SY, SZ = 8, 8, 128
ROW = SY * SZ
PROW = (SY + 2) * SZ
DIRS = [(1, 0), (-1, 0), (0, 1), (0, -1), (1, 1), (1, -1), (-1, 1), (-1, -1)]
NT = (((1,), (1,)), ((), ()))
NN = (((1,), (0,)), ((), ()))


def dot(a, b, dims):
    return lax.dot_general(a, b, dims, preferred_element_type=F32)


def lanes(shape):
    return lax.broadcasted_iota(jnp.int32, shape, 1)


def kernel(
    pg_ref, x_ref, wp_ref, out_ref, wg_ref,
    pg3, x12, pack, spread, gacc, dfull, acc,
    zsend, zrecv, xface, xroll,
    az, ax, wf, wk, wl,
    sx, rx, ef, ff, sy, ry, szf, rz,
    halo_s, halo_r, z_s, z_r, az_s, az_r, ay_s, ay_r, ax_s, ax_r,
    rx_s, rx_r, ry_s, ry_r, rz_s, rz_r,
):
    gx, gy, gz = lax.axis_index("gx"), lax.axis_index("gy"), lax.axis_index("gz")

    def send(src, dst, ss, rs, dev):
        return pltpu.make_async_remote_copy(
            src_ref=src, dst_ref=dst, send_sem=ss, recv_sem=rs, device_id=dev, device_id_type=MESH
        )

    barrier = pltpu.get_barrier_semaphore()
    for k in range(1, GX):
        pl.semaphore_signal(barrier, inc=1, device_id={"gx": lax.rem(gx + k, GX)}, device_id_type=MESH)
    for k in range(1, GY):
        pl.semaphore_signal(barrier, inc=1, device_id={"gy": lax.rem(gy + k, GY)}, device_id_type=MESH)
    for k in range(1, GZ):
        pl.semaphore_signal(barrier, inc=1, device_id={"gz": lax.rem(gz + k, GZ)}, device_id_type=MESH)
    for dx, dy in DIRS[4:]:
        pl.semaphore_signal(
            barrier,
            inc=1,
            device_id={"gx": lax.rem(gx + dx + GX, GX), "gy": lax.rem(gy + dy + GY, GY)},
            device_id_type=MESH,
        )

    pg3[1 : SX + 1, C : 2 * C, SZ : SZ + ROW] = pg_ref[...]
    x12[0 : 2 * C, :] = jnp.zeros((2 * C, ROW), BF)
    x12[(SX + 2) * C :, :] = jnp.zeros((2 * C, ROW), BF)
    for i in range(SX):
        x12[(i + 2) * C : (i + 3) * C, :] = x_ref[i]

    def where(d):
        sxd, syd = d
        if sxd == 1:
            sp, dp = pl.ds(SX - 1, 1), pl.ds(0, 1)
        elif sxd == -1:
            sp, dp = pl.ds(0, 1), pl.ds(SX + 1, 1)
        else:
            sp, dp = pl.ds(0, SX), pl.ds(1, SX)
        if syd == 1:
            sl, dl = pl.ds(ROW - SZ, SZ), pl.ds(0, SZ)
        elif syd == -1:
            sl, dl = pl.ds(0, SZ), pl.ds(PROW - SZ, SZ)
        else:
            sl, dl = pl.ds(0, ROW), pl.ds(SZ, ROW)
        return sp, sl, dp, dl

    def inside(dx, dy):
        return (gx + dx >= 0) & (gx + dx < GX) & (gy + dy >= 0) & (gy + dy < GY)

    def halo_copy(k):
        dx, dy = DIRS[k]
        sp, sl, dp, dl = where(DIRS[k])
        dev = {}
        if dx:
            dev["gx"] = gx + dx
        if dy:
            dev["gy"] = gy + dy
        return send(
            pg_ref.at[sp, :, sl], pg3.at[dp, pl.ds(C, C), dl], halo_s.at[k], halo_r.at[k], dev
        )

    for k, (dx, dy) in enumerate(DIRS):
        _, _, dp, dl = where((dx, dy))

        @pl.when(jnp.logical_not(inside(-dx, -dy)))
        def _(dp=dp, dl=dl):
            pg3[dp, C : 2 * C, dl] = jnp.zeros((dp.size, C, dl.size), BF)

    row = lax.broadcasted_iota(jnp.int32, (PROW, SZ), 0)
    col = lax.broadcasted_iota(jnp.int32, (PROW, SZ), 1)
    pack[:, 0:SZ] = jnp.where(row == col * SZ + SZ - 1, 1.0, 0.0).astype(BF)
    pack[:, SZ:] = jnp.where(row == col * SZ, 1.0, 0.0).astype(BF)
    row = lax.broadcasted_iota(jnp.int32, (SZ, PROW), 0)
    col = lax.broadcasted_iota(jnp.int32, (SZ, PROW), 1)
    spread[0] = jnp.where(col == row * SZ, 1.0, 0.0).astype(BF)
    spread[1] = jnp.where(col == row * SZ + SZ - 1, 1.0, 0.0).astype(BF)

    pl.semaphore_wait(barrier, GX + GY + GZ - 3 + 4)

    for k in range(1, GZ):
        send(wp_ref, az.at[k - 1], az_s.at[k - 1], az_r.at[k - 1], {"gz": lax.rem(gz + k, GZ)}).start()
    for k, (dx, dy) in enumerate(DIRS):

        @pl.when(inside(dx, dy))
        def _(k=k):
            halo_copy(k).start()

    xhi = jnp.zeros((C, SZ), F32)
    xlo = jnp.zeros((C, SZ), F32)
    for i in range(SX):
        t = dot(x_ref[i], pack[SZ : SZ + ROW, :], NN)
        xhi = xhi + pltpu.roll(t[:, :SZ], 10 * (i + 1), 1)
        xlo = xlo + pltpu.roll(t[:, SZ:], 10 * (i + 1), 1)
    for a in range(3):
        xroll[0, a * C : (a + 1) * C, :] = pltpu.roll(xhi, (-10 * (a - 1)) % SZ, 1).astype(BF)
        xroll[1, a * C : (a + 1) * C, :] = pltpu.roll(xlo, (-10 * (a - 1)) % SZ, 1).astype(BF)
    gacc[...] = jnp.zeros(gacc.shape, F32)
    acc[...] = jnp.zeros(acc.shape, F32)

    for k, (dx, dy) in enumerate(DIRS):

        @pl.when(inside(-dx, -dy))
        def _(k=k):
            halo_copy(k).wait_recv()

    xface[...] = jnp.zeros(xface.shape, F32)

    def pack_faces(px, carry):
        t = dot(pg3[px, C : 2 * C, :], pack[...], NN)
        xface[0] += pltpu.roll(t[:, :SZ], 10 * px, 1)
        xface[1] += pltpu.roll(t[:, SZ:], 10 * px, 1)
        return carry

    lax.fori_loop(0, SX + 2, pack_faces, 0)
    zsend[...] = xface[...].astype(BF)

    def z_copy(face):
        return send(
            zsend.at[face], zrecv.at[face], z_s.at[face], z_r.at[face], {"gz": gz + (1 - 2 * face)}
        )

    has = ((gz < GZ - 1), (gz > 0))
    for face in range(2):

        @pl.when(has[face])
        def _(face=face):
            z_copy(face).start()

        @pl.when(jnp.logical_not(has[1 - face]))
        def _(face=face):
            zrecv[face] = jnp.zeros((C, SZ), BF)

    for k in range(1, GZ):
        send(wp_ref, az.at[k - 1], az_s.at[k - 1], az_r.at[k - 1], {"gz": lax.rem(gz + k, GZ)}).wait()
    w = wp_ref[...].astype(F32)
    for k in range(GZ - 1):
        w = w + az[k].astype(F32)
    ax[gx, gy] = w.astype(BF)

    def ay_copy(k):
        return send(
            ax.at[gx, gy], ax.at[gx, gy], ay_s.at[k - 1], ay_r.at[k - 1], {"gy": lax.rem(gy + k, GY)}
        )

    for k in range(1, GY):
        ay_copy(k).start()

    lane = lanes((C, SZ))

    def shift(px, carry):
        for j in range(SY + 2):
            t = pg3[px, C : 2 * C, j * SZ : (j + 1) * SZ].astype(F32)
            up = jnp.where(lane == 0, 0.0, pltpu.roll(t, 1, 1))
            down = jnp.where(lane == SZ - 1, 0.0, pltpu.roll(t, SZ - 1, 1))
            pg3[px, 2 * C :, j * SZ : (j + 1) * SZ] = up.astype(BF)
            pg3[px, 0:C, j * SZ : (j + 1) * SZ] = down.astype(BF)
        return carry

    lax.fori_loop(0, SX + 2, shift, 0)

    def wgrad(px, carry):
        xs = x12[pl.ds(pl.multiple_of(px * C, C), 3 * C), :]
        for b in range(3):
            win = pg3[px, :, (2 - b) * SZ : (2 - b) * SZ + ROW]
            gacc[b, :, 0 : 3 * C] += dot(win, xs, NT)
        return carry

    lax.fori_loop(0, SX // 2 + 1, wgrad, 0)

    for k in range(1, GY):
        ay_copy(k).wait()

    def ax_copy(k):
        return send(ax.at[gx], ax.at[gx], ax_s.at[k - 1], ax_r.at[k - 1], {"gx": lax.rem(gx + k, GX)})

    for k in range(1, GX):
        ax_copy(k).start()

    lax.fori_loop(SX // 2 + 1, SX + 2, wgrad, 0)

    for face in range(2):

        @pl.when(has[1 - face])
        def _(face=face):
            z_copy(face).wait_recv()

    for face in range(2):
        c = 2 - 2 * face
        z = zrecv[face].astype(F32)
        for b in range(3):
            zb = pltpu.roll(z, (b - 1) % SZ, 1).astype(BF)
            gacc[b, c * C : (c + 1) * C, 0 : 3 * C] += dot(zb, xroll[1 - face], NT)

    half = lanes((C // 2, SZ)) < C
    dfull[27] = jnp.zeros((C // 2, SZ), F32)
    for b in range(3):
        for c in range(3):
            even, odd = c * C, c * C + C // 2
            e0, o0 = gacc[b, even:odd, 0:SZ], gacc[b, odd : odd + C // 2, 0:SZ]
            e1, o1 = gacc[b, even:odd, SZ:], gacc[b, odd : odd + C // 2, SZ:]
            t = b * 3 + c
            dfull[t] = jnp.where(half, e0, pltpu.roll(o0, C, 1))
            dfull[9 + t] = jnp.where(half, pltpu.roll(e0, C, 1), o0)
            dfull[18 + t] = jnp.where(half, e1, pltpu.roll(o1, C, 1))
    for u in range(14):
        for g in range(GX):
            pair = jnp.concatenate([dfull[2 * u, g * 8 : g * 8 + 8], dfull[2 * u + 1, g * 8 : g * 8 + 8]], 0)
            sx[g, u * 16 : (u + 1) * 16, :] = pair.astype(BF)

    def rx_copy(k):
        peer = lax.rem(gx + k, GX)
        return send(sx.at[peer], rx.at[k - 1], rx_s.at[k - 1], rx_r.at[k - 1], {"gx": peer})

    for k in range(1, GX):
        rx_copy(k).start()

    for k in range(1, GX):
        ax_copy(k).wait()
    for i in range(GX):
        for j in range(GY):
            r = (i * GY + j) * 32
            wf[r : r + 32, :] = ax[i, j].astype(F32)
    for b in range(3):
        wk[b, 3 * C :, :] = jnp.zeros((C, 2 * SZ), F32)
        for c in range(3):
            a0 = wf[pl.ds(b * 3 + c, 32, stride=32), :]
            a1 = wf[pl.ds(9 + b * 3 + c, 32, stride=32), :]
            a2 = wf[pl.ds(18 + b * 3 + c, 32, stride=32), :]
            r0, r1, r2 = (pltpu.roll(v, C, 1) for v in (a0, a1, a2))
            wk[b, c * C : c * C + 32, 0:SZ] = jnp.where(half, a0, r1)
            wk[b, c * C : c * C + 32, SZ:] = a2
            wk[b, c * C + 32 : c * C + 64, 0:SZ] = jnp.where(half, r0, a1)
            wk[b, c * C + 32 : c * C + 64, SZ:] = r2
        for m in range(2):
            for n in range(2):
                t = wk[b, n * SZ : (n + 1) * SZ, m * SZ : (m + 1) * SZ]
                wl[b, m * SZ : (m + 1) * SZ, n * SZ : (n + 1) * SZ] = t.T.astype(BF)

    xface[...] = zrecv[...].astype(F32)

    def patch(px, carry):
        back = lax.rem(SZ - 10 * px, SZ)
        for face in range(2):
            c = 2 - 2 * face
            t = pltpu.roll(xface[face], back, 1).astype(BF)
            put = dot(t, spread[face], NN)
            old = pg3[px, c * C : (c + 1) * C, :].astype(F32)
            pg3[px, c * C : (c + 1) * C, :] = (old + put).astype(BF)
        return carry

    lax.fori_loop(0, SX + 2, patch, 0)

    def dgrad(px, carry):
        at = pl.ds(pl.multiple_of(px * C, C), 3 * C)
        for n in range(4):
            y = None
            for b in range(3):
                lo = (2 - b) * SZ + n * 256
                d = dot(wl[b, 0 : 3 * C, 0 : 3 * C], pg3[px, :, lo : lo + 256], NN)
                y = d if y is None else y + d
            acc[at, n * 256 : (n + 1) * 256] += y
        return carry

    lax.fori_loop(0, 4, dgrad, 0)

    for k in range(1, GX):
        rx_copy(k).wait()
    mine = pl.ds(pl.multiple_of(gx * 8, 8), 8)
    for u in range(14):
        v = jnp.concatenate([dfull[2 * u, mine, :], dfull[2 * u + 1, mine, :]], 0)
        for k in range(GX - 1):
            v = v + rx[k, u * 16 : (u + 1) * 16, :].astype(F32)
        ef[u * 16 : (u + 1) * 16, :] = v
    ef[224:, :] = jnp.zeros((32, SZ), F32)
    for g in range(GY):
        v = ef[pl.ds(g, 32, stride=8), :]
        ff[g] = v
        sy[g] = v.astype(BF)

    def ry_copy(k):
        peer = lax.rem(gy + k, GY)
        return send(sy.at[peer], ry.at[k - 1], ry_s.at[k - 1], ry_r.at[k - 1], {"gy": peer})

    for k in range(1, GY):
        ry_copy(k).start()

    lax.fori_loop(4, 7, dgrad, 0)

    for k in range(1, GY):
        ry_copy(k).wait()
    v = ff[gy]
    for k in range(GY - 1):
        v = v + ry[k].astype(F32)
    v = jnp.concatenate([v, jnp.zeros((96, SZ), F32)], 0)
    szf[...] = v.T

    def rz_copy(k):
        peer = lax.rem(gz + k, GZ)
        return send(
            szf.at[pl.ds(pl.multiple_of(peer * 16, 16), 16), :], rz.at[k - 1], rz_s.at[k - 1], rz_r.at[k - 1], {"gz": peer}
        )

    for k in range(1, GZ):
        rz_copy(k).start()

    lax.fori_loop(7, SX + 2, dgrad, 0)
    for i in range(SX):
        out_ref[i] = acc[(i + 2) * C : (i + 3) * C, :].astype(BF)

    for k in range(1, GZ):
        rz_copy(k).wait()
    v = szf[pl.ds(pl.multiple_of(gz * 16, 16), 16), :]
    for k in range(GZ - 1):
        v = v + rz[k]
    wg_ref[...] = v

    for k, (dx, dy) in enumerate(DIRS):

        @pl.when(inside(dx, dy))
        def _(k=k):
            halo_copy(k).wait_send()

    for face in range(2):

        @pl.when(has[face])
        def _(face=face):
            z_copy(face).wait_send()


def call(pg, x, wp):
    vmem = pl.BlockSpec(memory_space=pltpu.VMEM)
    dma = pltpu.SemaphoreType.DMA
    v = pltpu.VMEM
    return pl.pallas_call(
        kernel,
        out_shape=(
            jax.ShapeDtypeStruct((SX, C, ROW), BF),
            jax.ShapeDtypeStruct((16, SZ), F32),
        ),
        in_specs=[vmem] * 3,
        out_specs=(vmem, vmem),
        scratch_shapes=[
            v((SX + 2, 3 * C, PROW), BF),
            v(((SX + 4) * C, ROW), BF),
            v((PROW, 2 * SZ), BF),
            v((2, SZ, PROW), BF),
            v((3, 3 * C, 2 * SZ), F32),
            v((28, C // 2, SZ), F32),
            v(((SX + 4) * C, ROW), F32),
            v((2, C, SZ), BF),
            v((2, C, SZ), BF),
            v((2, C, SZ), F32),
            v((2, 3 * C, SZ), BF),
            v((GZ - 1, 32, SZ), BF),
            v((GX, GY, 32, SZ), BF),
            v((1024, SZ), F32),
            v((3, 2 * SZ, 2 * SZ), F32),
            v((3, 2 * SZ, 2 * SZ), BF),
            v((GX, 224, SZ), BF),
            v((GX - 1, 224, SZ), BF),
            v((256, SZ), F32),
            v((GY, 32, SZ), F32),
            v((GY, 32, SZ), BF),
            v((GY - 1, 32, SZ), BF),
            v((SZ, SZ), F32),
            v((GZ - 1, 16, SZ), F32),
            dma((8,)), dma((8,)), dma((2,)), dma((2,)),
            dma((GZ - 1,)), dma((GZ - 1,)), dma((GY - 1,)), dma((GY - 1,)), dma((GX - 1,)), dma((GX - 1,)),
            dma((GX - 1,)), dma((GX - 1,)), dma((GY - 1,)), dma((GY - 1,)), dma((GZ - 1,)), dma((GZ - 1,)),
        ],
        compiler_params=pltpu.CompilerParams(
            collective_id=0, has_side_effects=True, vmem_limit_bytes=56 * 1024 * 1024
        ),
    )(pg, x, wp)


def local(activations, preact, upstream, master, first_moment, second_moment):
    pre_grad = jnp.where(preact > 0, upstream, jnp.zeros_like(upstream))
    pg = jnp.transpose(pre_grad.reshape(C // 2, 2, SX, SY, SZ), (2, 1, 0, 3, 4)).reshape(SX, C, ROW)
    x = jnp.transpose(activations, (1, 0, 2, 3)).reshape(SX, C, ROW)
    w = jnp.pad(master.astype(BF).reshape(16, 27).T, ((0, 5), (0, 0)))
    own = lax.broadcasted_iota(jnp.int32, (32, SZ), 1) // 16 == lax.axis_index("gz")
    wp = jnp.where(own, jnp.tile(w, (1, 8)), jnp.zeros((), BF))
    out, wg = call(pg, x, wp)
    grad_input = jnp.transpose(out.reshape(SX, C, SY, SZ), (1, 0, 2, 3))
    voxels = SX * SY * SZ * GX * GY * GZ
    weight_grad = wg[:, :27].reshape(-1) / math.sqrt(voxels)
    new_first = 0.9 * first_moment + 0.1 * weight_grad
    new_second = 0.999 * second_moment + 0.001 * weight_grad * weight_grad
    corr_first = 1.0 - (0.9**10) ** 10
    corr_second = 1.0 - (0.999**10) ** 10
    update = new_first / corr_first / (jnp.sqrt(new_second / corr_second) + 1e-08) + 0.01 * master
    new_master = master - 0.05 * update
    return (grad_input, weight_grad, new_master, new_first, new_second)


def solution(mesh):
    vol = P(None, "gx", "gy", "gz")
    par = P(("gx", "gy", "gz"))
    return jax.shard_map(
        local,
        mesh=mesh,
        in_specs=(vol, vol, vol, par, par, par),
        out_specs=(vol, par, par, par, par),
        check_vma=False,
    )
```

```python
import functools
import math

import jax
import jax.numpy as jnp
from jax import lax
from jax.experimental import pallas as pl
from jax.experimental.pallas import tpu as pltpu
from jax.sharding import PartitionSpec as P

MESH = pl.DeviceIdType.MESH
TRACE = False
_scope = [None]
BF, F32 = jnp.bfloat16, jnp.float32
GX, GY, GZ = 4, 8, 8
C = 64
SX, SY, SZ = 8, 8, 128
ROW = SY * SZ
PROW = (SY + 2) * SZ
DIRS = [(1, 0), (-1, 0), (0, 1), (0, -1), (1, 1), (1, -1), (-1, 1), (-1, -1)]
NT = (((1,), (1,)), ((), ()))
NN = (((1,), (0,)), ((), ()))


def dot(a, b, dims):
    return lax.dot_general(a, b, dims, preferred_element_type=F32)


def mark(name):
    if not TRACE:
        return
    if _scope[0] is not None:
        _scope[0].__exit__(None, None, None)
        _scope[0] = None
    if name:
        _scope[0] = jax.named_scope(name)
        _scope[0].__enter__()


def lanes(shape):
    return lax.broadcasted_iota(jnp.int32, shape, 1)


def kernel(
    pg_ref, x_ref, wp_ref, out_ref, wg_ref,
    pg3, x3, pack, spread, gacc, dfull, acc,
    zsend, zrecv, xsend, xrecv,
    az, ax, wf, wk, wl,
    sx, rx, ef, ff, sy, ry, szf, rz,
    halo_s, halo_r, z_s, z_r, xz_s, xz_r, az_s, az_r, ay_s, ay_r, ax_s, ax_r,
    rx_s, rx_r, ry_s, ry_r, rz_s, rz_r,
):
    gx, gy, gz = lax.axis_index("gx"), lax.axis_index("gy"), lax.axis_index("gz")

    def send(src, dst, ss, rs, dev):
        return pltpu.make_async_remote_copy(
            src_ref=src, dst_ref=dst, send_sem=ss, recv_sem=rs, device_id=dev, device_id_type=MESH
        )

    mark("barsig")
    barrier = pltpu.get_barrier_semaphore()
    for k in range(1, GX):
        pl.semaphore_signal(barrier, inc=1, device_id={"gx": lax.rem(gx + k, GX)}, device_id_type=MESH)
    for k in range(1, GY):
        pl.semaphore_signal(barrier, inc=1, device_id={"gy": lax.rem(gy + k, GY)}, device_id_type=MESH)
    for k in range(1, GZ):
        pl.semaphore_signal(barrier, inc=1, device_id={"gz": lax.rem(gz + k, GZ)}, device_id_type=MESH)
    for dx, dy in DIRS[4:]:
        pl.semaphore_signal(
            barrier,
            inc=1,
            device_id={"gx": lax.rem(gx + dx + GX, GX), "gy": lax.rem(gy + dy + GY, GY)},
            device_id_type=MESH,
        )

    mark("prep")
    pg3[1 : SX + 1, C : 2 * C, SZ : SZ + ROW] = pg_ref[...]

    def where(d):
        sxd, syd = d
        if sxd == 1:
            sp, dp = pl.ds(SX - 1, 1), pl.ds(0, 1)
        elif sxd == -1:
            sp, dp = pl.ds(0, 1), pl.ds(SX + 1, 1)
        else:
            sp, dp = pl.ds(0, SX), pl.ds(1, SX)
        if syd == 1:
            sl, dl = pl.ds(ROW - SZ, SZ), pl.ds(0, SZ)
        elif syd == -1:
            sl, dl = pl.ds(0, SZ), pl.ds(PROW - SZ, SZ)
        else:
            sl, dl = pl.ds(0, ROW), pl.ds(SZ, ROW)
        return sp, sl, dp, dl

    def inside(dx, dy):
        return (gx + dx >= 0) & (gx + dx < GX) & (gy + dy >= 0) & (gy + dy < GY)

    def halo_copy(k):
        dx, dy = DIRS[k]
        sp, sl, dp, dl = where(DIRS[k])
        dev = {}
        if dx:
            dev["gx"] = gx + dx
        if dy:
            dev["gy"] = gy + dy
        return send(
            pg_ref.at[sp, :, sl], pg3.at[dp, pl.ds(C, C), dl], halo_s.at[k], halo_r.at[k], dev
        )

    for k, (dx, dy) in enumerate(DIRS):
        _, _, dp, dl = where((dx, dy))

        @pl.when(jnp.logical_not(inside(-dx, -dy)))
        def _(dp=dp, dl=dl):
            pg3[dp, C : 2 * C, dl] = jnp.zeros((dp.size, C, dl.size), BF)

    row = lax.broadcasted_iota(jnp.int32, (PROW, SZ), 0)
    col = lax.broadcasted_iota(jnp.int32, (PROW, SZ), 1)
    pack[:, 0:SZ] = jnp.where(row == col * SZ + SZ - 1, 1.0, 0.0).astype(BF)
    pack[:, SZ:] = jnp.where(row == col * SZ, 1.0, 0.0).astype(BF)

    has = ((gz < GZ - 1), (gz > 0))

    def faces(planes, first):
        n = planes.shape[0]
        t = dot(planes.reshape(n * C, planes.shape[2]), pack[0 : planes.shape[2], :], NN)
        high = jnp.zeros((C, SZ), F32)
        low = jnp.zeros((C, SZ), F32)
        for i in range(n):
            high = high + pltpu.roll(t[i * C : (i + 1) * C, :SZ], 10 * i, 1)
            low = low + pltpu.roll(t[i * C : (i + 1) * C, SZ:], 10 * i, 1)
        return high, low

    def x_copy(face):
        return send(
            xsend.at[face], xrecv.at[face], xz_s.at[face], xz_r.at[face], {"gz": gz + (1 - 2 * face)}
        )

    def z_copy(face):
        return send(
            zsend.at[face], zrecv.at[face], z_s.at[face], z_r.at[face], {"gz": gz + (1 - 2 * face)}
        )

    mark("xfaces")
    high, low = faces(x_ref[...], 0)
    xsend[0] = high.astype(BF)
    xsend[1] = low.astype(BF)

    mark("barwait")
    pl.semaphore_wait(barrier, GX + GY + GZ - 3 + 4)

    mark("start")
    for k, (dx, dy) in enumerate(DIRS):

        @pl.when(inside(dx, dy))
        def _(k=k):
            halo_copy(k).start()

    for face in range(2):

        @pl.when(has[face])
        def _(face=face):
            x_copy(face).start()

        @pl.when(jnp.logical_not(has[1 - face]))
        def _(face=face):
            xrecv[face] = jnp.zeros((C, SZ), BF)

    for k in range(1, GZ):
        send(wp_ref, az.at[k - 1], az_s.at[k - 1], az_r.at[k - 1], {"gz": lax.rem(gz + k, GZ)}).start()

    mark("xshift")
    lane = lanes((C, SZ))
    gacc[...] = jnp.zeros(gacc.shape, F32)

    def xshift(i, carry):
        x3[i, C : 2 * C, :] = x_ref[i]
        for j in range(SY):
            t = x_ref[i, :, j * SZ : (j + 1) * SZ].astype(F32)
            up = jnp.where(lane == 0, 0.0, pltpu.roll(t, 1, 1))
            down = jnp.where(lane == SZ - 1, 0.0, pltpu.roll(t, SZ - 1, 1))
            x3[i, 0:C, j * SZ : (j + 1) * SZ] = up.astype(BF)
            x3[i, 2 * C :, j * SZ : (j + 1) * SZ] = down.astype(BF)
        return carry

    lax.fori_loop(0, SX, xshift, 0)

    CUT = ((256, 0, 896), (128, 0, 1024), (128, 128, 896))

    def wdot(plane, n, q, b, lo):
        ps, xo, size = CUT[b]
        win = pg3[pl.ds(plane, n), C : 2 * C, ps : ps + size].reshape(n * C, size)
        gacc[b, lo * C : (lo + n) * C, 0 : 3 * C] += dot(win, x3[q, :, xo : xo + size], NT)

    def wgrad(q, carry):
        for b in range(3):
            wdot(q, 3, q, b, 0)
        return carry

    mark("wgrad")
    lax.fori_loop(1, SX - 1, wgrad, 0)
    for b in range(3):
        wdot(1, 2, 0, b, 1)
        wdot(SX - 1, 2, SX - 1, b, 0)
    acc[...] = jnp.zeros(acc.shape, F32)

    mark("halowait")
    for k, (dx, dy) in enumerate(DIRS):

        @pl.when(inside(-dx, -dy))
        def _(k=k):
            halo_copy(k).wait_recv()

    mark("pgfaces")
    zhigh, zlow = faces(pg3[:, C : 2 * C, :], 0)
    zsend[0] = zhigh.astype(BF)
    zsend[1] = zlow.astype(BF)
    for face in range(2):

        @pl.when(has[face])
        def _(face=face):
            z_copy(face).start()

        @pl.when(jnp.logical_not(has[1 - face]))
        def _(face=face):
            zrecv[face] = jnp.zeros((C, SZ), BF)

    mark("azwait")
    for k in range(1, GZ):
        send(wp_ref, az.at[k - 1], az_s.at[k - 1], az_r.at[k - 1], {"gz": lax.rem(gz + k, GZ)}).wait()
    w = wp_ref[...].astype(F32)
    for k in range(GZ - 1):
        w = w + az[k].astype(F32)
    ax[gx, gy] = w.astype(BF)

    def ay_copy(k):
        return send(
            ax.at[gx, gy], ax.at[gx, gy], ay_s.at[k - 1], ay_r.at[k - 1], {"gy": lax.rem(gy + k, GY)}
        )

    for k in range(1, GY):
        ay_copy(k).start()

    mark("wedge")
    for b in range(3):
        wdot(0, 1, 0, b, 0)
        wdot(SX + 1, 1, SX - 1, b, 2)
    for b, ps, xo in ((2, 0, 0), (0, PROW - SZ, ROW - SZ)):
        y = None
        for q in range(0, SX, 2):
            left = [pg3[v : v + 3, C : 2 * C, ps : ps + SZ].reshape(3 * C, SZ) for v in (q, q + 1)]
            right = [x3[v, :, xo : xo + SZ] for v in (q, q + 1)]
            d = dot(jnp.concatenate(left, 1), jnp.concatenate(right, 1), NT)
            y = d if y is None else y + d
        gacc[b, :, 0 : 3 * C] += y

    mark("xzwait")
    for face in range(2):

        @pl.when(has[1 - face])
        def _(face=face):
            x_copy(face).wait_recv()

    mark("zcorr")
    for face, local in ((0, zlow), (1, zhigh)):
        c = 2 * face
        for b in range(3):
            rows = [pltpu.roll(local, (-(10 * j + 2 - b)) % SZ, 1) for j in range(3)]
            rows = jnp.concatenate(rows, 0).astype(BF)
            gacc[b, :, c * C : (c + 1) * C] += dot(rows, xrecv[face], NT)

    mark("dfull")
    half = lanes((C // 2, SZ)) < C
    dfull[27] = jnp.zeros((C // 2, SZ), F32)
    for b in range(3):
        for a in range(3):
            even = (2 - a) * C
            odd = even + C // 2
            e0, o0 = gacc[b, even:odd, 0:SZ], gacc[b, odd : odd + C // 2, 0:SZ]
            e1, o1 = gacc[b, even:odd, SZ:], gacc[b, odd : odd + C // 2, SZ:]
            t = a * 9 + b * 3
            dfull[t] = jnp.where(half, e0, pltpu.roll(o0, C, 1))
            dfull[t + 1] = jnp.where(half, pltpu.roll(e0, C, 1), o0)
            dfull[t + 2] = jnp.where(half, e1, pltpu.roll(o1, C, 1))
    for u in range(14):
        for g in range(GX):
            pair = jnp.concatenate([dfull[2 * u, g * 8 : g * 8 + 8], dfull[2 * u + 1, g * 8 : g * 8 + 8]], 0)
            sx[g, u * 16 : (u + 1) * 16, :] = pair.astype(BF)

    def rx_copy(k):
        peer = lax.rem(gx + k, GX)
        return send(sx.at[peer], rx.at[k - 1], rx_s.at[k - 1], rx_r.at[k - 1], {"gx": peer})

    for k in range(1, GX):
        rx_copy(k).start()

    def shift(px, carry):
        for j in range(SY + 2):
            t = pg3[px, C : 2 * C, j * SZ : (j + 1) * SZ].astype(F32)
            up = jnp.where(lane == 0, 0.0, pltpu.roll(t, 1, 1))
            down = jnp.where(lane == SZ - 1, 0.0, pltpu.roll(t, SZ - 1, 1))
            pg3[px, 2 * C :, j * SZ : (j + 1) * SZ] = up.astype(BF)
            pg3[px, 0:C, j * SZ : (j + 1) * SZ] = down.astype(BF)
        return carry

    mark("shift1")
    lax.fori_loop(0, 5, shift, 0)

    mark("aywait")
    for k in range(1, GY):
        ay_copy(k).wait()

    def ax_copy(k):
        return send(ax.at[gx], ax.at[gx], ax_s.at[k - 1], ax_r.at[k - 1], {"gx": lax.rem(gx + k, GX)})

    for k in range(1, GX):
        ax_copy(k).start()

    mark("shift2")
    lax.fori_loop(5, SX + 2, shift, 0)
    row = lax.broadcasted_iota(jnp.int32, (SZ, PROW), 0)
    col = lax.broadcasted_iota(jnp.int32, (SZ, PROW), 1)
    spread[0] = jnp.where(col == row * SZ, 1.0, 0.0).astype(BF)
    spread[1] = jnp.where(col == row * SZ + SZ - 1, 1.0, 0.0).astype(BF)

    mark("zwait")
    for face in range(2):

        @pl.when(has[1 - face])
        def _(face=face):
            z_copy(face).wait_recv()

    mark("patch")
    for face in range(2):
        c = 2 - 2 * face
        z = zrecv[face].astype(F32)
        rows = [pltpu.roll(z, (-10 * i) % SZ, 1) for i in range(SX + 2)]
        rows = jnp.concatenate(rows, 0).astype(BF)
        for n in range(5):
            put = dot(rows, spread[face, :, n * 256 : (n + 1) * 256], NN).reshape(SX + 2, C, 256)
            old = pg3[:, c * C : (c + 1) * C, n * 256 : (n + 1) * 256].astype(F32)
            pg3[:, c * C : (c + 1) * C, n * 256 : (n + 1) * 256] = (old + put).astype(BF)

    mark("rxwait")
    for k in range(1, GX):
        rx_copy(k).wait()
    mark("rxsum")
    mine = pl.ds(pl.multiple_of(gx * 8, 8), 8)
    for u in range(14):
        v = jnp.concatenate([dfull[2 * u, mine, :], dfull[2 * u + 1, mine, :]], 0)
        for k in range(GX - 1):
            v = v + rx[k, u * 16 : (u + 1) * 16, :].astype(F32)
        ef[u * 16 : (u + 1) * 16, :] = v
    ef[224:, :] = jnp.zeros((32, SZ), F32)
    for g in range(GY):
        v = ef[pl.ds(g, 32, stride=8), :]
        ff[g] = v
        sy[g] = v.astype(BF)

    def ry_copy(k):
        peer = lax.rem(gy + k, GY)
        return send(sy.at[peer], ry.at[k - 1], ry_s.at[k - 1], ry_r.at[k - 1], {"gy": peer})

    for k in range(1, GY):
        ry_copy(k).start()

    mark("axwait")
    for k in range(1, GX):
        ax_copy(k).wait()
    mark("wk")
    for i in range(GX):
        for j in range(GY):
            r = (i * GY + j) * 32
            wf[r : r + 32, :] = ax[i, j].astype(F32)
    for b in range(3):
        wk[b, 3 * C :, :] = jnp.zeros((C, 2 * SZ), F32)
        for c in range(3):
            a0 = wf[pl.ds(b * 3 + c, 32, stride=32), :]
            a1 = wf[pl.ds(9 + b * 3 + c, 32, stride=32), :]
            a2 = wf[pl.ds(18 + b * 3 + c, 32, stride=32), :]
            r0, r1, r2 = (pltpu.roll(v, C, 1) for v in (a0, a1, a2))
            wk[b, c * C : c * C + 32, 0:SZ] = jnp.where(half, a0, r1)
            wk[b, c * C : c * C + 32, SZ:] = a2
            wk[b, c * C + 32 : c * C + 64, 0:SZ] = jnp.where(half, r0, a1)
            wk[b, c * C + 32 : c * C + 64, SZ:] = r2
        for m in range(2):
            for n in range(2):
                t = wk[b, n * SZ : (n + 1) * SZ, m * SZ : (m + 1) * SZ]
                wl[b, m * SZ : (m + 1) * SZ, n * SZ : (n + 1) * SZ] = t.T.astype(BF)

    def dgrad(px, carry):
        at = pl.ds(pl.multiple_of(px * C, C), 3 * C)
        for n in range(4):
            y = None
            for b in range(3):
                lo = (2 - b) * SZ + n * 256
                d = dot(wl[b, 0 : 3 * C, 0 : 3 * C], pg3[px, :, lo : lo + 256], NN)
                y = d if y is None else y + d
            acc[at, n * 256 : (n + 1) * 256] += y
        return carry

    mark("dgrad1")
    lax.fori_loop(0, 4, dgrad, 0)

    mark("rywait")
    for k in range(1, GY):
        ry_copy(k).wait()
    mark("rysum")
    v = ff[gy]
    for k in range(GY - 1):
        v = v + ry[k].astype(F32)
    v = jnp.concatenate([v, jnp.zeros((96, SZ), F32)], 0)
    szf[...] = v.T

    def rz_copy(k):
        peer = lax.rem(gz + k, GZ)
        return send(
            szf.at[pl.ds(pl.multiple_of(peer * 16, 16), 16), :], rz.at[k - 1], rz_s.at[k - 1], rz_r.at[k - 1], {"gz": peer}
        )

    for k in range(1, GZ):
        rz_copy(k).start()

    mark("dgrad2")
    lax.fori_loop(4, SX + 2, dgrad, 0)
    for i in range(SX):
        out_ref[i] = acc[(i + 2) * C : (i + 3) * C, :].astype(BF)

    mark("rzwait")
    for k in range(1, GZ):
        rz_copy(k).wait()
    mark("end")
    v = szf[pl.ds(pl.multiple_of(gz * 16, 16), 16), :]
    for k in range(GZ - 1):
        v = v + rz[k]
    wg_ref[...] = v

    for k, (dx, dy) in enumerate(DIRS):

        @pl.when(inside(dx, dy))
        def _(k=k):
            halo_copy(k).wait_send()

    for face in range(2):

        @pl.when(has[face])
        def _(face=face):
            z_copy(face).wait_send()
            x_copy(face).wait_send()

    mark(None)


def call(pg, x, wp):
    vmem = pl.BlockSpec(memory_space=pltpu.VMEM)
    dma = pltpu.SemaphoreType.DMA
    v = pltpu.VMEM
    return pl.pallas_call(
        kernel,
        out_shape=(
            jax.ShapeDtypeStruct((SX, C, ROW), BF),
            jax.ShapeDtypeStruct((16, SZ), F32),
        ),
        in_specs=[vmem] * 3,
        out_specs=(vmem, vmem),
        scratch_shapes=[
            v((SX + 2, 3 * C, PROW), BF),
            v((SX, 3 * C, ROW), BF),
            v((PROW, 2 * SZ), BF),
            v((2, SZ, PROW), BF),
            v((3, 3 * C, 2 * SZ), F32),
            v((28, C // 2, SZ), F32),
            v(((SX + 4) * C, ROW), F32),
            v((2, C, SZ), BF),
            v((2, C, SZ), BF),
            v((2, C, SZ), BF),
            v((2, C, SZ), BF),
            v((GZ - 1, 32, SZ), BF),
            v((GX, GY, 32, SZ), BF),
            v((1024, SZ), F32),
            v((3, 2 * SZ, 2 * SZ), F32),
            v((3, 2 * SZ, 2 * SZ), BF),
            v((GX, 224, SZ), BF),
            v((GX - 1, 224, SZ), BF),
            v((256, SZ), F32),
            v((GY, 32, SZ), F32),
            v((GY, 32, SZ), BF),
            v((GY - 1, 32, SZ), BF),
            v((SZ, SZ), F32),
            v((GZ - 1, 16, SZ), F32),
            dma((8,)), dma((8,)), dma((2,)), dma((2,)), dma((2,)), dma((2,)),
            dma((GZ - 1,)), dma((GZ - 1,)), dma((GY - 1,)), dma((GY - 1,)), dma((GX - 1,)), dma((GX - 1,)),
            dma((GX - 1,)), dma((GX - 1,)), dma((GY - 1,)), dma((GY - 1,)), dma((GZ - 1,)), dma((GZ - 1,)),
        ],
        compiler_params=pltpu.CompilerParams(
            collective_id=0, has_side_effects=True, vmem_limit_bytes=56 * 1024 * 1024
        ),
    )(pg, x, wp)


def local(activations, preact, upstream, master, first_moment, second_moment):
    pre_grad = jnp.where(preact > 0, upstream, jnp.zeros_like(upstream))
    pg = jnp.transpose(pre_grad.reshape(C // 2, 2, SX, SY, SZ), (2, 1, 0, 3, 4)).reshape(SX, C, ROW)
    x = jnp.transpose(activations, (1, 0, 2, 3)).reshape(SX, C, ROW)
    w = jnp.pad(master.astype(BF).reshape(16, 27).T, ((0, 5), (0, 0)))
    own = lax.broadcasted_iota(jnp.int32, (32, SZ), 1) // 16 == lax.axis_index("gz")
    wp = jnp.where(own, jnp.tile(w, (1, 8)), jnp.zeros((), BF))
    out, wg = call(pg, x, wp)
    grad_input = jnp.transpose(out.reshape(SX, C, SY, SZ), (1, 0, 2, 3))
    voxels = SX * SY * SZ * GX * GY * GZ
    weight_grad = wg[:, :27].reshape(-1) / math.sqrt(voxels)
    new_first = 0.9 * first_moment + 0.1 * weight_grad
    new_second = 0.999 * second_moment + 0.001 * weight_grad * weight_grad
    corr_first = 1.0 - (0.9**10) ** 10
    corr_second = 1.0 - (0.999**10) ** 10
    update = new_first / corr_first / (jnp.sqrt(new_second / corr_second) + 1e-08) + 0.01 * master
    new_master = master - 0.05 * update
    return (grad_input, weight_grad, new_master, new_first, new_second)


def solution(mesh):
    vol = P(None, "gx", "gy", "gz")
    par = P(("gx", "gy", "gz"))
    return jax.shard_map(
        local,
        mesh=mesh,
        in_specs=(vol, vol, vol, par, par, par),
        out_specs=(vol, par, par, par, par),
        check_vma=False,
    )
```

```python
import functools
import math

import jax
import jax.numpy as jnp
from jax import lax
from jax.experimental import pallas as pl
from jax.experimental.pallas import tpu as pltpu
from jax.sharding import PartitionSpec as P

MESH = pl.DeviceIdType.MESH
TRACE = False
_scope = [None]
BF, F32 = jnp.bfloat16, jnp.float32
GX, GY, GZ = 4, 8, 8
C = 64
SX, SY, SZ = 8, 8, 128
ROW = SY * SZ
PROW = (SY + 2) * SZ
NCH = 4
CHUNK = C * SX * SY // NCH
DIRS = [(1, 0), (-1, 0), (0, 1), (0, -1), (1, 1), (1, -1), (-1, 1), (-1, -1)]
NT = (((1,), (1,)), ((), ()))
NN = (((1,), (0,)), ((), ()))


def dot(a, b, dims):
    return lax.dot_general(a, b, dims, preferred_element_type=F32)


def mark(name):
    if not TRACE:
        return
    if _scope[0] is not None:
        _scope[0].__exit__(None, None, None)
        _scope[0] = None
    if name:
        _scope[0] = jax.named_scope(name)
        _scope[0].__enter__()


def lanes(shape):
    return lax.broadcasted_iota(jnp.int32, shape, 1)


def kernel(
    pre_ref, up_ref, act_ref, m_ref, out_ref, wg_ref,
    pbuf, ubuf, xbuf, nat, wt, wp_ref, in_s, out_s,
    pg3, x3, pack, spread, gacc, dfull, acc,
    zsend, zrecv, xsend, xrecv,
    az, ax, wf, wk, wl,
    sx, rx, ef, ff, sy, ry, szf, rz,
    halo_s, halo_r, z_s, z_r, xz_s, xz_r, az_s, az_r, ay_s, ay_r, ax_s, ax_r,
    rx_s, rx_r, ry_s, ry_r, rz_s, rz_r,
):
    gx, gy, gz = lax.axis_index("gx"), lax.axis_index("gy"), lax.axis_index("gz")

    def send(src, dst, ss, rs, dev):
        return pltpu.make_async_remote_copy(
            src_ref=src, dst_ref=dst, send_sem=ss, recv_sem=rs, device_id=dev, device_id_type=MESH
        )

    def fetch(src, dst, i, n):
        at = pl.ds(i * CHUNK, CHUNK)
        return pltpu.make_async_copy(src.at[at, :], dst.at[at, :], in_s.at[n, i])

    for i in range(NCH):
        fetch(pre_ref, pbuf, i, 0).start()
        fetch(up_ref, ubuf, i, 1).start()
    for i in range(NCH):
        fetch(act_ref, xbuf, i, 2).start()

    mark("barsig")
    barrier = pltpu.get_barrier_semaphore()
    for k in range(1, GX):
        pl.semaphore_signal(barrier, inc=1, device_id={"gx": lax.rem(gx + k, GX)}, device_id_type=MESH)
    for k in range(1, GY):
        pl.semaphore_signal(barrier, inc=1, device_id={"gy": lax.rem(gy + k, GY)}, device_id_type=MESH)
    for k in range(1, GZ):
        pl.semaphore_signal(barrier, inc=1, device_id={"gz": lax.rem(gz + k, GZ)}, device_id_type=MESH)
    for dx, dy in DIRS[4:]:
        pl.semaphore_signal(
            barrier,
            inc=1,
            device_id={"gx": lax.rem(gx + dx + GX, GX), "gy": lax.rem(gy + dy + GY, GY)},
            device_id_type=MESH,
        )

    mark("prep")
    wt[...] = jnp.zeros(wt.shape, F32)
    wt[pl.ds(pl.multiple_of(gz * 16, 16), 16), 0:27] = m_ref[...]
    wp_ref[...] = wt[...].T[0:32, :].astype(BF)

    def where(d):
        sxd, syd = d
        if sxd == 1:
            sp, dp = pl.ds(SX, 1), pl.ds(0, 1)
        elif sxd == -1:
            sp, dp = pl.ds(1, 1), pl.ds(SX + 1, 1)
        else:
            sp, dp = pl.ds(1, SX), pl.ds(1, SX)
        if syd == 1:
            sl, dl = pl.ds(ROW, SZ), pl.ds(0, SZ)
        elif syd == -1:
            sl, dl = pl.ds(SZ, SZ), pl.ds(PROW - SZ, SZ)
        else:
            sl, dl = pl.ds(SZ, ROW), pl.ds(SZ, ROW)
        return sp, sl, dp, dl

    def inside(dx, dy):
        return (gx + dx >= 0) & (gx + dx < GX) & (gy + dy >= 0) & (gy + dy < GY)

    def halo_copy(k):
        dx, dy = DIRS[k]
        sp, sl, dp, dl = where(DIRS[k])
        dev = {}
        if dx:
            dev["gx"] = gx + dx
        if dy:
            dev["gy"] = gy + dy
        return send(
            pg3.at[sp, pl.ds(C, C), sl], pg3.at[dp, pl.ds(C, C), dl], halo_s.at[k], halo_r.at[k], dev
        )

    for k, (dx, dy) in enumerate(DIRS):
        _, _, dp, dl = where((dx, dy))

        @pl.when(jnp.logical_not(inside(-dx, -dy)))
        def _(dp=dp, dl=dl):
            pg3[dp, C : 2 * C, dl] = jnp.zeros((dp.size, C, dl.size), BF)

    row = lax.broadcasted_iota(jnp.int32, (PROW, SZ), 0)
    col = lax.broadcasted_iota(jnp.int32, (PROW, SZ), 1)
    pack[:, 0:SZ] = jnp.where(row == col * SZ + SZ - 1, 1.0, 0.0).astype(BF)
    pack[:, SZ:] = jnp.where(row == col * SZ, 1.0, 0.0).astype(BF)

    has = ((gz < GZ - 1), (gz > 0))

    def faces(planes, first):
        n = planes.shape[0]
        t = dot(planes.reshape(n * C, planes.shape[2]), pack[0 : planes.shape[2], :], NN)
        high = jnp.zeros((C, SZ), F32)
        low = jnp.zeros((C, SZ), F32)
        for i in range(n):
            high = high + pltpu.roll(t[i * C : (i + 1) * C, :SZ], 10 * i, 1)
            low = low + pltpu.roll(t[i * C : (i + 1) * C, SZ:], 10 * i, 1)
        return high, low

    def x_copy(face):
        return send(
            xsend.at[face], xrecv.at[face], xz_s.at[face], xz_r.at[face], {"gz": gz + (1 - 2 * face)}
        )

    def z_copy(face):
        return send(
            zsend.at[face], zrecv.at[face], z_s.at[face], z_r.at[face], {"gz": gz + (1 - 2 * face)}
        )

    mark("pgin")
    for i in range(NCH):
        fetch(pre_ref, pbuf, i, 0).wait()
        fetch(up_ref, ubuf, i, 1).wait()

        def select(r, carry, i=i):
            at = pl.ds(pl.multiple_of(i * CHUNK + r * 128, 128), 128)
            u = ubuf[at, :].astype(F32)
            nat[at, :] = jnp.where(pbuf[at, :].astype(F32) > 0.0, u, 0.0)
            return carry

        lax.fori_loop(0, CHUNK // 128, select, 0)

    def pgplane(i, carry):
        for j in range(SY):
            at = i * SY + j
            to = pl.ds((j + 1) * SZ, SZ)
            pg3[i + 1, C : C + C // 2, to] = nat[pl.ds(at, C // 2, stride=128), :].astype(BF)
            pg3[i + 1, C + C // 2 : 2 * C, to] = nat[pl.ds(at + 64, C // 2, stride=128), :].astype(BF)
        return carry

    lax.fori_loop(0, SX, pgplane, 0)

    mark("xin")
    for i in range(NCH):
        fetch(act_ref, xbuf, i, 2).wait()

    def widen(r, carry):
        at = pl.ds(pl.multiple_of(r * 128, 128), 128)
        nat[at, :] = xbuf[at, :].astype(F32)
        return carry

    lax.fori_loop(0, C * SX * SY // 128, widen, 0)
    lane = lanes((C, SZ))

    def xplane(i, carry):
        for j in range(SY):
            t = nat[pl.ds(i * SY + j, C, stride=64), :]
            up = jnp.where(lane == 0, 0.0, pltpu.roll(t, 1, 1))
            down = jnp.where(lane == SZ - 1, 0.0, pltpu.roll(t, SZ - 1, 1))
            x3[i, C : 2 * C, j * SZ : (j + 1) * SZ] = t.astype(BF)
            x3[i, 0:C, j * SZ : (j + 1) * SZ] = up.astype(BF)
            x3[i, 2 * C :, j * SZ : (j + 1) * SZ] = down.astype(BF)
        return carry

    lax.fori_loop(0, SX, xplane, 0)
    gacc[...] = jnp.zeros(gacc.shape, F32)

    mark("xfaces")
    high, low = faces(x3[:, C : 2 * C, :], 0)
    xsend[0] = high.astype(BF)
    xsend[1] = low.astype(BF)

    mark("barwait")
    pl.semaphore_wait(barrier, GX + GY + GZ - 3 + 4)

    mark("start")
    for k, (dx, dy) in enumerate(DIRS):

        @pl.when(inside(dx, dy))
        def _(k=k):
            halo_copy(k).start()

    for face in range(2):

        @pl.when(has[face])
        def _(face=face):
            x_copy(face).start()

        @pl.when(jnp.logical_not(has[1 - face]))
        def _(face=face):
            xrecv[face] = jnp.zeros((C, SZ), BF)

    for k in range(1, GZ):
        send(wp_ref, az.at[k - 1], az_s.at[k - 1], az_r.at[k - 1], {"gz": lax.rem(gz + k, GZ)}).start()

    CUT = ((256, 0, 896), (128, 0, 1024), (128, 128, 896))

    def wdot(plane, n, q, b, lo):
        ps, xo, size = CUT[b]
        win = pg3[pl.ds(plane, n), C : 2 * C, ps : ps + size].reshape(n * C, size)
        gacc[b, lo * C : (lo + n) * C, 0 : 3 * C] += dot(win, x3[q, :, xo : xo + size], NT)

    def wgrad(q, carry):
        for b in range(3):
            wdot(q, 3, q, b, 0)
        return carry

    mark("wgrad")
    lax.fori_loop(1, SX - 1, wgrad, 0)
    for b in range(3):
        wdot(1, 2, 0, b, 1)
        wdot(SX - 1, 2, SX - 1, b, 0)
    acc[...] = jnp.zeros(acc.shape, F32)

    mark("halowait")
    for k, (dx, dy) in enumerate(DIRS):

        @pl.when(inside(-dx, -dy))
        def _(k=k):
            halo_copy(k).wait_recv()

    mark("pgfaces")
    zhigh, zlow = faces(pg3[:, C : 2 * C, :], 0)
    zsend[0] = zhigh.astype(BF)
    zsend[1] = zlow.astype(BF)
    for face in range(2):

        @pl.when(has[face])
        def _(face=face):
            z_copy(face).start()

        @pl.when(jnp.logical_not(has[1 - face]))
        def _(face=face):
            zrecv[face] = jnp.zeros((C, SZ), BF)

    mark("azwait")
    for k in range(1, GZ):
        send(wp_ref, az.at[k - 1], az_s.at[k - 1], az_r.at[k - 1], {"gz": lax.rem(gz + k, GZ)}).wait()
    w = wp_ref[...].astype(F32)
    for k in range(GZ - 1):
        w = w + az[k].astype(F32)
    ax[gx, gy] = w.astype(BF)

    def ay_copy(k):
        return send(
            ax.at[gx, gy], ax.at[gx, gy], ay_s.at[k - 1], ay_r.at[k - 1], {"gy": lax.rem(gy + k, GY)}
        )

    for k in range(1, GY):
        ay_copy(k).start()

    mark("wedge")
    for b in range(3):
        wdot(0, 1, 0, b, 0)
        wdot(SX + 1, 1, SX - 1, b, 2)
    for b, ps, xo in ((2, 0, 0), (0, PROW - SZ, ROW - SZ)):
        y = None
        for q in range(0, SX, 2):
            left = [pg3[v : v + 3, C : 2 * C, ps : ps + SZ].reshape(3 * C, SZ) for v in (q, q + 1)]
            right = [x3[v, :, xo : xo + SZ] for v in (q, q + 1)]
            d = dot(jnp.concatenate(left, 1), jnp.concatenate(right, 1), NT)
            y = d if y is None else y + d
        gacc[b, :, 0 : 3 * C] += y

    mark("xzwait")
    for face in range(2):

        @pl.when(has[1 - face])
        def _(face=face):
            x_copy(face).wait_recv()

    mark("zcorr")
    for face, local in ((0, zlow), (1, zhigh)):
        c = 2 * face
        for b in range(3):
            rows = [pltpu.roll(local, (-(10 * j + 2 - b)) % SZ, 1) for j in range(3)]
            rows = jnp.concatenate(rows, 0).astype(BF)
            gacc[b, :, c * C : (c + 1) * C] += dot(rows, xrecv[face], NT)

    mark("dfull")
    half = lanes((C // 2, SZ)) < C
    dfull[27] = jnp.zeros((C // 2, SZ), F32)
    for b in range(3):
        for a in range(3):
            even = (2 - a) * C
            odd = even + C // 2
            e0, o0 = gacc[b, even:odd, 0:SZ], gacc[b, odd : odd + C // 2, 0:SZ]
            e1, o1 = gacc[b, even:odd, SZ:], gacc[b, odd : odd + C // 2, SZ:]
            t = a * 9 + b * 3
            dfull[t] = jnp.where(half, e0, pltpu.roll(o0, C, 1))
            dfull[t + 1] = jnp.where(half, pltpu.roll(e0, C, 1), o0)
            dfull[t + 2] = jnp.where(half, e1, pltpu.roll(o1, C, 1))
    for u in range(14):
        for g in range(GX):
            pair = jnp.concatenate([dfull[2 * u, g * 8 : g * 8 + 8], dfull[2 * u + 1, g * 8 : g * 8 + 8]], 0)
            sx[g, u * 16 : (u + 1) * 16, :] = pair.astype(BF)

    def rx_copy(k):
        peer = lax.rem(gx + k, GX)
        return send(sx.at[peer], rx.at[k - 1], rx_s.at[k - 1], rx_r.at[k - 1], {"gx": peer})

    for k in range(1, GX):
        rx_copy(k).start()

    def shift(px, carry):
        for j in range(SY + 2):
            t = pg3[px, C : 2 * C, j * SZ : (j + 1) * SZ].astype(F32)
            up = jnp.where(lane == 0, 0.0, pltpu.roll(t, 1, 1))
            down = jnp.where(lane == SZ - 1, 0.0, pltpu.roll(t, SZ - 1, 1))
            pg3[px, 2 * C :, j * SZ : (j + 1) * SZ] = up.astype(BF)
            pg3[px, 0:C, j * SZ : (j + 1) * SZ] = down.astype(BF)
        return carry

    mark("shift1")
    lax.fori_loop(0, 5, shift, 0)

    mark("aywait")
    for k in range(1, GY):
        ay_copy(k).wait()

    def ax_copy(k):
        return send(ax.at[gx], ax.at[gx], ax_s.at[k - 1], ax_r.at[k - 1], {"gx": lax.rem(gx + k, GX)})

    for k in range(1, GX):
        ax_copy(k).start()

    mark("shift2")
    lax.fori_loop(5, SX + 2, shift, 0)
    row = lax.broadcasted_iota(jnp.int32, (SZ, PROW), 0)
    col = lax.broadcasted_iota(jnp.int32, (SZ, PROW), 1)
    spread[0] = jnp.where(col == row * SZ, 1.0, 0.0).astype(BF)
    spread[1] = jnp.where(col == row * SZ + SZ - 1, 1.0, 0.0).astype(BF)

    mark("zwait")
    for face in range(2):

        @pl.when(has[1 - face])
        def _(face=face):
            z_copy(face).wait_recv()

    mark("patch")
    for face in range(2):
        c = 2 - 2 * face
        z = zrecv[face].astype(F32)
        rows = [pltpu.roll(z, (-10 * i) % SZ, 1) for i in range(SX + 2)]
        rows = jnp.concatenate(rows, 0).astype(BF)
        for n in range(5):
            put = dot(rows, spread[face, :, n * 256 : (n + 1) * 256], NN).reshape(SX + 2, C, 256)
            old = pg3[:, c * C : (c + 1) * C, n * 256 : (n + 1) * 256].astype(F32)
            pg3[:, c * C : (c + 1) * C, n * 256 : (n + 1) * 256] = (old + put).astype(BF)

    mark("rxwait")
    for k in range(1, GX):
        rx_copy(k).wait()
    mark("rxsum")
    mine = pl.ds(pl.multiple_of(gx * 8, 8), 8)
    for u in range(14):
        v = jnp.concatenate([dfull[2 * u, mine, :], dfull[2 * u + 1, mine, :]], 0)
        for k in range(GX - 1):
            v = v + rx[k, u * 16 : (u + 1) * 16, :].astype(F32)
        ef[u * 16 : (u + 1) * 16, :] = v
    ef[224:, :] = jnp.zeros((32, SZ), F32)
    for g in range(GY):
        v = ef[pl.ds(g, 32, stride=8), :]
        ff[g] = v
        sy[g] = v.astype(BF)

    def ry_copy(k):
        peer = lax.rem(gy + k, GY)
        return send(sy.at[peer], ry.at[k - 1], ry_s.at[k - 1], ry_r.at[k - 1], {"gy": peer})

    for k in range(1, GY):
        ry_copy(k).start()

    mark("axwait")
    for k in range(1, GX):
        ax_copy(k).wait()
    mark("wk")
    for i in range(GX):
        for j in range(GY):
            r = (i * GY + j) * 32
            wf[r : r + 32, :] = ax[i, j].astype(F32)
    for b in range(3):
        wk[b, 3 * C :, :] = jnp.zeros((C, 2 * SZ), F32)
        for c in range(3):
            a0 = wf[pl.ds(b * 3 + c, 32, stride=32), :]
            a1 = wf[pl.ds(9 + b * 3 + c, 32, stride=32), :]
            a2 = wf[pl.ds(18 + b * 3 + c, 32, stride=32), :]
            r0, r1, r2 = (pltpu.roll(v, C, 1) for v in (a0, a1, a2))
            wk[b, c * C : c * C + 32, 0:SZ] = jnp.where(half, a0, r1)
            wk[b, c * C : c * C + 32, SZ:] = a2
            wk[b, c * C + 32 : c * C + 64, 0:SZ] = jnp.where(half, r0, a1)
            wk[b, c * C + 32 : c * C + 64, SZ:] = r2
        for m in range(2):
            for n in range(2):
                t = wk[b, n * SZ : (n + 1) * SZ, m * SZ : (m + 1) * SZ]
                wl[b, m * SZ : (m + 1) * SZ, n * SZ : (n + 1) * SZ] = t.T.astype(BF)

    def dgrad(px, carry):
        at = pl.ds(pl.multiple_of(px * C, C), 3 * C)
        for n in range(4):
            y = None
            for b in range(3):
                lo = (2 - b) * SZ + n * 256
                d = dot(wl[b, 0 : 3 * C, 0 : 3 * C], pg3[px, :, lo : lo + 256], NN)
                y = d if y is None else y + d
            acc[at, n * 256 : (n + 1) * 256] += y
        return carry

    mark("dgrad1")
    lax.fori_loop(0, 4, dgrad, 0)

    mark("rywait")
    for k in range(1, GY):
        ry_copy(k).wait()
    mark("rysum")
    v = ff[gy]
    for k in range(GY - 1):
        v = v + ry[k].astype(F32)
    v = jnp.concatenate([v, jnp.zeros((96, SZ), F32)], 0)
    szf[...] = v.T

    def rz_copy(k):
        peer = lax.rem(gz + k, GZ)
        return send(
            szf.at[pl.ds(pl.multiple_of(peer * 16, 16), 16), :], rz.at[k - 1], rz_s.at[k - 1], rz_r.at[k - 1], {"gz": peer}
        )

    for k in range(1, GZ):
        rz_copy(k).start()

    mark("dgrad2")
    lax.fori_loop(4, SX + 2, dgrad, 0)
    mark("out")

    def oplane(i, carry):
        at = pl.ds(pl.multiple_of((i + 2) * C, C), C)
        for j in range(SY):
            nat[pl.ds(i * SY + j, C, stride=64), :] = acc[at, j * SZ : (j + 1) * SZ]
        return carry

    lax.fori_loop(0, SX, oplane, 0)

    def emit(i):
        at = pl.ds(i * CHUNK, CHUNK)
        return pltpu.make_async_copy(ubuf.at[at, :], out_ref.at[at, :], out_s.at[i])

    for i in range(NCH):

        def narrow(r, carry, i=i):
            at = pl.ds(pl.multiple_of(i * CHUNK + r * 128, 128), 128)
            ubuf[at, :] = nat[at, :].astype(BF)
            return carry

        lax.fori_loop(0, CHUNK // 128, narrow, 0)
        emit(i).start()

    mark("rzwait")
    for k in range(1, GZ):
        rz_copy(k).wait()
    mark("end")
    v = szf[pl.ds(pl.multiple_of(gz * 16, 16), 16), :]
    for k in range(GZ - 1):
        v = v + rz[k]
    wg_ref[...] = v
    for i in range(NCH):
        emit(i).wait()

    for k, (dx, dy) in enumerate(DIRS):

        @pl.when(inside(dx, dy))
        def _(k=k):
            halo_copy(k).wait_send()

    for face in range(2):

        @pl.when(has[face])
        def _(face=face):
            z_copy(face).wait_send()
            x_copy(face).wait_send()

    mark(None)


def call(pre, up, act, m):
    vmem = pl.BlockSpec(memory_space=pltpu.VMEM)
    hbm = pl.BlockSpec(memory_space=pl.ANY)
    dma = pltpu.SemaphoreType.DMA
    v = pltpu.VMEM
    n = C * SX * SY
    return pl.pallas_call(
        kernel,
        out_shape=(
            jax.ShapeDtypeStruct((n, SZ), BF),
            jax.ShapeDtypeStruct((16, SZ), F32),
        ),
        in_specs=[hbm, hbm, hbm, vmem],
        out_specs=(hbm, vmem),
        scratch_shapes=[
            v((n, SZ), BF), v((n, SZ), BF), v((n, SZ), BF), v((n, SZ), F32),
            v((SZ, SZ), F32), v((32, SZ), BF), dma((3, NCH)), dma((NCH,)),
            v((SX + 2, 3 * C, PROW), BF),
            v((SX, 3 * C, ROW), BF),
            v((PROW, 2 * SZ), BF),
            v((2, SZ, PROW), BF),
            v((3, 3 * C, 2 * SZ), F32),
            v((28, C // 2, SZ), F32),
            v(((SX + 4) * C, ROW), F32),
            v((2, C, SZ), BF),
            v((2, C, SZ), BF),
            v((2, C, SZ), BF),
            v((2, C, SZ), BF),
            v((GZ - 1, 32, SZ), BF),
            v((GX, GY, 32, SZ), BF),
            v((1024, SZ), F32),
            v((3, 2 * SZ, 2 * SZ), F32),
            v((3, 2 * SZ, 2 * SZ), BF),
            v((GX, 224, SZ), BF),
            v((GX - 1, 224, SZ), BF),
            v((256, SZ), F32),
            v((GY, 32, SZ), F32),
            v((GY, 32, SZ), BF),
            v((GY - 1, 32, SZ), BF),
            v((SZ, SZ), F32),
            v((GZ - 1, 16, SZ), F32),
            dma((8,)), dma((8,)), dma((2,)), dma((2,)), dma((2,)), dma((2,)),
            dma((GZ - 1,)), dma((GZ - 1,)), dma((GY - 1,)), dma((GY - 1,)), dma((GX - 1,)), dma((GX - 1,)),
            dma((GX - 1,)), dma((GX - 1,)), dma((GY - 1,)), dma((GY - 1,)), dma((GZ - 1,)), dma((GZ - 1,)),
        ],
        compiler_params=pltpu.CompilerParams(
            collective_id=0, has_side_effects=True, vmem_limit_bytes=56 * 1024 * 1024
        ),
    )(pre, up, act, m)


def local(activations, preact, upstream, master, first_moment, second_moment):
    flat = [v.reshape(C * SX * SY, SZ) for v in (preact, upstream, activations)]
    out, wg = call(*flat, master.reshape(16, 27))
    grad_input = out.reshape(C, SX, SY, SZ)
    voxels = SX * SY * SZ * GX * GY * GZ
    weight_grad = wg[:, :27].reshape(-1) / math.sqrt(voxels)
    new_first = 0.9 * first_moment + 0.1 * weight_grad
    new_second = 0.999 * second_moment + 0.001 * weight_grad * weight_grad
    corr_first = 1.0 - (0.9**10) ** 10
    corr_second = 1.0 - (0.999**10) ** 10
    update = new_first / corr_first / (jnp.sqrt(new_second / corr_second) + 1e-08) + 0.01 * master
    new_master = master - 0.05 * update
    return (grad_input, weight_grad, new_master, new_first, new_second)


def solution(mesh):
    vol = P(None, "gx", "gy", "gz")
    par = P(("gx", "gy", "gz"))
    return jax.shard_map(
        local,
        mesh=mesh,
        in_specs=(vol, vol, vol, par, par, par),
        out_specs=(vol, par, par, par, par),
        check_vma=False,
    )
```
